32 devices in a mesh: segment: 4 (over z), expert: 4 (over y, core), token: 2 (over x).
Axes of the slice: x: 2, y: 2, z: 4, core: 2. Of those that a mesh axis runs over, the one named last changes fastest.
Arguments:
- fwd_acts: bfloat16 [4, 256, 2048], P('segment', 'expert'), may hold values from -6 to 6
- fwd_ids: int32 [4, 256, 6], P('segment', 'expert'), may hold values from 0 to 7, as said below
- fwd_slots: int32 [4, 256, 6], P('segment', 'expert'), may hold values from 0 to 36, as said below
- bwd_acts: bfloat16 [4, 256, 2048], P('segment', 'expert'), may hold values from -6 to 6
- bwd_ids: int32 [4, 256, 6], P('segment', 'expert'), may hold values from 0 to 7, as said below
- bwd_slots: int32 [4, 256, 6], P('segment', 'expert'), may hold values from 0 to 36, as said below
- bwd_grad: bfloat16 [4, 256, 2048], P('segment', 'expert'), may hold values from -6 to 6
- norm_gain: float32 [4, 2048], P('segment'), may hold values from 0.25 to 1.75
- router: float32 [4, 2048, 8], P('segment'), may hold values from -0.125 to 0.125
- w_gate: bfloat16 [8, 2048, 1408], P('expert', None, 'token'), may hold values from -0.125 to 0.125
- w_up: bfloat16 [8, 2048, 1408], P('expert', None, 'token'), may hold values from -0.125 to 0.125
- w_down: bfloat16 [8, 1408, 2048], P('expert', 'token'), may hold values from -0.15625 to 0.15625
Outputs:
- next_acts: bfloat16 [4, 256, 2048], P('segment', 'expert', 'token')
- prev_grads: bfloat16 [4, 256, 2048], P('segment', 'expert', 'token')
The draws below stay inside these ranges and needn't reach their ends.
Inputs may be any that keep to these rules, and one draw needn't show every extreme that they name: `fwd_ids`: each row names 6 different experts. `fwd_slots`: entry (t, k) counts the assignments to expert fwd_ids[t, k] that come before it in t's block of 64 rows (rows in order, a row's 6 choices in order), capped at 36; 36 marks a dropped assignment. In every block one expert, the same for all blocks of a section, is named by more than 36 rows. `bwd_ids`: each row names 6 different experts. `bwd_slots`: entry (t, k) counts the assignments to expert bwd_ids[t, k] that come before it in t's block of 64 rows (rows in order, a row's 6 choices in order), capped at 36; 36 marks a dropped assignment. In every block one expert, the same for all blocks of a section, is named by more than 36 rows.
All inputs are finite; a program needn't handle non-finite values.
Results may differ from the reference program's by a relative error of at most 0.009.
Values may be sent and summed in bfloat16 or wider, within the bound.
A program may use at most 128 MiB of HBM per device.

```python
import jax
import jax.numpy as jnp
from jax import lax

D = 2048
FF = 1408
TOPK = 6
TOK_DEV = 64
SEGMENTS = 4
EXPERTS = 8
CAP = 36
TOKENS = 256
N_TOKEN = 2


def route_table(key):
    blocks = TOKENS // TOK_DEV
    key_hot, key_base, key_count, key_order = jax.random.split(key, 4)
    hottest = jax.random.randint(key_hot, (SEGMENTS, 1, 1, 1), 0, EXPERTS)
    columns = jnp.arange(EXPERTS, dtype=jnp.int32)
    scores = jax.random.randint(key_base, (SEGMENTS, blocks, TOK_DEV, EXPERTS), 0, 65536) * EXPERTS + columns
    counts = jax.random.randint(key_count, (SEGMENTS, blocks, 1), CAP + 1, TOK_DEV + 1)
    order_keys = jax.random.randint(key_order, (SEGMENTS, blocks, TOK_DEV), 0, 1048576) * TOK_DEV + jnp.arange(TOK_DEV, dtype=jnp.int32)
    ranking = jnp.argsort(jnp.argsort(order_keys, axis=-1), axis=-1)
    forced = ranking < counts
    scores = jnp.where(forced[..., None] & (columns == hottest), 1073741824, scores)
    _, chosen = lax.top_k(scores, TOPK)
    flattened = chosen.reshape(SEGMENTS, blocks, TOK_DEV * TOPK)
    onehot = (flattened[..., None] == columns).astype(jnp.int32)
    before = jnp.cumsum(onehot, axis=2) - onehot
    slot_ids = jnp.minimum(jnp.sum(before * onehot, axis=-1), CAP)
    return (chosen.reshape(SEGMENTS, TOKENS, TOPK).astype(jnp.int32), slot_ids.reshape(SEGMENTS, TOKENS, TOPK).astype(jnp.int32))


def draw_fwd_ids(key, part):
    return route_table(jax.random.fold_in(key, 17))[0]


def draw_fwd_slots(key, part):
    return route_table(jax.random.fold_in(key, 17))[1]


def draw_bwd_ids(key, part):
    return route_table(jax.random.fold_in(key, 29))[0]


def draw_bwd_slots(key, part):
    return route_table(jax.random.fold_in(key, 29))[1]


def steps_of(rng, extent, cuts, least, top_value):
    loudness = 1.0
    for axis_at, blocks in cuts:
        heights = jax.random.uniform(jax.random.fold_in(jax.random.fold_in(rng, 6), axis_at), (blocks,), jnp.float32, least / len(cuts), top_value / len(cuts))
        loudness = loudness * jnp.repeat(jnp.exp(heights), extent[axis_at] // blocks).reshape((-1,) + (1,) * (len(extent) - 1 - axis_at))
    return loudness


def normal_values(rng, dims, scale, most, cuts=(), kind=jnp.bfloat16):
    values = scale * jax.random.normal(rng, dims, jnp.float32)
    if cuts:
        values = values * steps_of(rng, dims, cuts, -0.22, 0.18)
    return jnp.clip(values, -most, most).astype(kind)


def setup_inputs(seed: int = 0) -> dict:
    streams_of = jax.random.split(jax.random.key(seed), 13)
    return {
        "fwd_acts": normal_values(streams_of[0], (SEGMENTS, TOKENS, D), 1.0, 6.0, ((0, 4), (1, 4))),
        "fwd_ids": draw_fwd_ids(jax.random.fold_in(streams_of[12], 71), 0),
        "fwd_slots": draw_fwd_slots(jax.random.fold_in(streams_of[12], 71), 0),
        "bwd_acts": normal_values(streams_of[3], (SEGMENTS, TOKENS, D), 1.0, 6.0, ((0, 4), (1, 4))),
        "bwd_ids": draw_bwd_ids(jax.random.fold_in(streams_of[12], 71), 0),
        "bwd_slots": draw_bwd_slots(jax.random.fold_in(streams_of[12], 71), 0),
        "bwd_grad": normal_values(streams_of[6], (SEGMENTS, TOKENS, D), 1.0, 6.0, ((0, 4), (1, 4))),
        "norm_gain": jnp.clip(1.0 + 0.15 * jax.random.normal(streams_of[7], (SEGMENTS, D), jnp.float32), 0.25, 1.75),
        "router": normal_values(streams_of[8], (SEGMENTS, D, EXPERTS), D ** -0.5, 0.125, ((0, 4),), jnp.float32),
        "w_gate": normal_values(streams_of[9], (EXPERTS, D, FF), D ** -0.5, 0.125, ((0, 4), (2, 2))),
        "w_up": normal_values(streams_of[10], (EXPERTS, D, FF), D ** -0.5, 0.125, ((0, 4), (2, 2))),
        "w_down": normal_values(streams_of[11], (EXPERTS, FF, D), FF ** -0.5, 0.15625, ((0, 4), (1, 2))),
    }


route_scale = 2.446
norm_eps = 1e-06
highest = lax.Precision.HIGHEST

def normalize(values, norm_scale):
    widened = values.astype(jnp.float32)
    inverse = lax.rsqrt(lax.optimization_barrier(jnp.mean(widened * widened, axis=-1, keepdims=True)) + norm_eps)
    scaled = widened * inverse
    return ((scaled * norm_scale).astype(jnp.bfloat16), scaled, inverse)

def gating(normed, expert_ids, router):
    logits = jnp.dot(normed.astype(jnp.float32), router, precision=highest)
    sigmoids = jax.nn.sigmoid(logits)
    picked = (expert_ids[..., None] == jnp.arange(router.shape[1], dtype=jnp.int32)).astype(jnp.float32)
    chosen = lax.optimization_barrier(jnp.sum(picked * sigmoids[..., None, :], axis=-1))
    totals = lax.optimization_barrier(jnp.sum(chosen, axis=-1, keepdims=True))
    return (route_scale * chosen / totals, chosen, totals, picked)

def finish(fwd_rows, mixed_fwd, normed_b, scaled_b, inverse_b, ids_b, cotangent, mixed_back, grad_gates, norm_scale, router):
    next_rows = (fwd_rows.astype(jnp.float32) + mixed_fwd).astype(jnp.bfloat16)
    gates_b, chosen, totals, picked = gating(normed_b, ids_b, router)
    grad_probs = route_scale * grad_gates / totals - route_scale * lax.optimization_barrier(jnp.sum(grad_gates * chosen, axis=-1, keepdims=True)) / (totals * totals)
    grad_logit = grad_probs * chosen * (1.0 - chosen)
    dense_grad = lax.optimization_barrier(jnp.sum(picked * grad_logit[..., None], axis=-2))
    grad_norm = mixed_back + jnp.dot(dense_grad, router.T, precision=highest)
    grad_scaled = grad_norm * norm_scale
    grad_in = inverse_b * (grad_scaled - scaled_b * lax.optimization_barrier(jnp.mean(grad_scaled * scaled_b, axis=-1, keepdims=True)))
    prev_rows = (cotangent.astype(jnp.float32) + grad_in).astype(jnp.bfloat16)
    return (next_rows, prev_rows)

def part_sum(pieces):
    rounded = lax.optimization_barrier(pieces.astype(jnp.bfloat16))
    return lax.optimization_barrier(jnp.sum(rounded.astype(jnp.float32), axis=0))

def expert_block(pieces):
    rows_fwd, rows_saved, rows_cot, gate_w, up_w, down_w = pieces
    count_rows = rows_fwd.shape[0]
    split_down = down_w.reshape(N_TOKEN, -1, down_w.shape[1]).astype(jnp.float32)
    split_gate_w = gate_w.reshape(gate_w.shape[0], N_TOKEN, -1).astype(jnp.float32)
    split_up_w = up_w.reshape(up_w.shape[0], N_TOKEN, -1).astype(jnp.float32)

    def down_parts(active):
        split_act = active.reshape(count_rows, N_TOKEN, -1).astype(jnp.float32)
        return part_sum(jnp.einsum('rnf,nfd->nrd', split_act, split_down, precision=highest))
    gate_fwd = jnp.dot(rows_fwd, gate_w, preferred_element_type=jnp.float32)
    up_fwd = jnp.dot(rows_fwd, up_w, preferred_element_type=jnp.float32)
    active = (gate_fwd * jax.nn.sigmoid(gate_fwd) * up_fwd).astype(jnp.bfloat16)
    out_fwd = down_parts(active)
    gate_bwd = jnp.dot(rows_saved, gate_w, preferred_element_type=jnp.float32)
    up_bwd = jnp.dot(rows_saved, up_w, preferred_element_type=jnp.float32)
    sigma = jax.nn.sigmoid(gate_bwd)
    active_bwd = (gate_bwd * sigma * up_bwd).astype(jnp.bfloat16)
    out_bwd = down_parts(active_bwd)
    grad_act = jnp.dot(rows_cot, down_w.T, preferred_element_type=jnp.float32)
    grad_gate = (grad_act * up_bwd * sigma * (1.0 + gate_bwd * (1.0 - sigma))).astype(jnp.bfloat16)
    grad_up = (grad_act * gate_bwd * sigma).astype(jnp.bfloat16)
    split_gg = grad_gate.reshape(count_rows, N_TOKEN, -1).astype(jnp.float32)
    split_gu = grad_up.reshape(count_rows, N_TOKEN, -1).astype(jnp.float32)
    back_pieces = jnp.einsum('rnf,dnf->nrd', split_gg, split_gate_w, precision=highest) + jnp.einsum('rnf,dnf->nrd', split_gu, split_up_w, precision=highest)
    back_in = part_sum(back_pieces)
    return (out_fwd, out_bwd, back_in)

def reference(fwd_acts, fwd_ids, fwd_slots, bwd_acts, bwd_ids, bwd_slots, bwd_grad, norm_gain, router, w_gate, w_up, w_down):
    blocks = TOKENS // TOK_DEV
    rows_per = blocks * CAP
    holder = EXPERTS * rows_per
    block_of = (jnp.arange(TOKENS, dtype=jnp.int32) // TOK_DEV)[:, None]

    def placing(expert_ids, slot_ids):
        return jnp.where(slot_ids < CAP, (expert_ids * blocks + block_of) * CAP + slot_ids, holder).astype(jnp.int32)

    def fill_buffer(token_rows, place):
        spread = jnp.repeat(token_rows, TOPK, axis=0)
        blank_rows = jnp.zeros((holder + 1, D), token_rows.dtype)
        filled = blank_rows.at[place.reshape(-1)].set(spread)
        return filled[:holder].reshape(EXPERTS, rows_per, D)

    def lookup(values, place):
        flattened = jnp.concatenate((values.reshape(holder, D), jnp.zeros((1, D), jnp.float32)), axis=0)
        return flattened[place]

    def segment_layer(inputs):
        fwd_x, ids_a, slots_a, bwd_x, ids_b, slots_b, cotangent, norm_scale, segment_router = inputs
        normed_a, _, _ = normalize(fwd_x, norm_scale)
        normed_b, scaled_b, inverse_b = normalize(bwd_x, norm_scale)
        place_a = placing(ids_a, slots_a)
        place_b = placing(ids_b, slots_b)
        buffer_a = fill_buffer(normed_a, place_a)
        buffer_b = fill_buffer(normed_b, place_b)
        buffer_c = fill_buffer(cotangent, place_b)
        out_fwd, out_bwd, back_in = lax.map(expert_block, (buffer_a, buffer_b, buffer_c, w_gate, w_up, w_down))
        gates_a = gating(normed_a, ids_a, segment_router)[0]
        gates_b = gating(normed_b, ids_b, segment_router)[0]
        mixed_fwd = lax.optimization_barrier(jnp.sum(gates_a[..., None] * lookup(out_fwd, place_a), axis=1))
        mixed_back = lax.optimization_barrier(jnp.sum(gates_b[..., None] * lookup(back_in, place_b), axis=1))
        grad_gates = lax.optimization_barrier(jnp.sum(cotangent.astype(jnp.float32)[:, None, :] * lookup(out_bwd, place_b), axis=-1))
        return finish(fwd_x, mixed_fwd, normed_b, scaled_b, inverse_b, ids_b, cotangent, mixed_back, grad_gates, norm_scale, segment_router)
    next_all, prev_all = lax.map(segment_layer, (fwd_acts, fwd_ids, fwd_slots, bwd_acts, bwd_ids, bwd_slots, bwd_grad, norm_gain, router))
    zero_block = jnp.zeros((1, TOKENS, D), next_all.dtype)
    next_acts = jnp.concatenate((zero_block, next_all[:-1]), axis=0)
    prev_grads = jnp.concatenate((prev_all[1:], zero_block), axis=0)
    return (next_acts, prev_grads)
```

```python
import functools

import jax
import jax.numpy as jnp
from jax import lax
from jax.experimental import pallas as pl
from jax.experimental.pallas import tpu as pltpu
from jax.sharding import PartitionSpec as P

route_scale = 2.446
norm_eps = 1e-06
highest = lax.Precision.HIGHEST
MESH = pl.DeviceIdType.MESH
f32 = jnp.float32
bf16 = jnp.bfloat16
NT = (((1,), (1,)), ((), ()))
NN = (((1,), (0,)), ((), ()))


def mm(a, b, dims=NN):
    return lax.dot_general(a, b, dims, preferred_element_type=f32)


def kernel(
    sizes,
    fa,
    ba,
    bg,
    codes,
    gain,
    router_t,
    wg_h,
    wu_h,
    wd_h,
    out_next,
    out_prev,
    X,
    N,
    G,
    wg,
    wu,
    wd,
    gg,
    gu,
    Pb,
    R1,
    Q,
    R2,
    Z,
    R3,
    Sc,
    Sb,
    RS,
    DGT,
    own,
    zbuf,
    w_sem,
    l_sem,
    s0,
    r0,
    s1,
    r1,
    sg,
    rg,
    ssib,
    rsib,
    stok,
    rtok,
    sR1,
    rR1,
    sR2,
    rR2,
    sR3,
    rR3,
    sS,
    rS,
    sz,
    rz,
):
    n_seg, n_e, n_t, per, E, tok, D, F, K = sizes
    J = n_e // 2
    W = D // n_t
    T = n_e * tok
    seg = lax.axis_index("segment")
    me = lax.axis_index("expert")
    x = lax.axis_index("token")
    k = lax.rem(me, 2)
    j0 = me // 2
    sib = j0 * 2 + 1 - k

    def cols(share):
        return pl.ds(pl.multiple_of(share * W, 128), W)

    def rcopy(src, dst, ss, rs, dev):
        return pltpu.make_async_remote_copy(
            src_ref=src, dst_ref=dst, send_sem=ss, recv_sem=rs, device_id=dev, device_id_type=MESH
        )

    started = []

    def go(copy):
        copy.start()
        started.append(copy)
        return copy

    ins = (fa, ba, bg)
    local = []
    for s in range(3):
        c = pltpu.make_async_copy(ins[s].at[0], X.at[s, k, j0], l_sem.at[s])
        c.start()
        local.append(c)
    weights = []
    for i, (h, v) in enumerate(((wg_h, wg), (wu_h, wu), (wd_h, wd))):
        c = pltpu.make_async_copy(h, v, w_sem.at[i])
        c.start()
        weights.append(c)

    barrier = pltpu.get_barrier_semaphore()
    for de in range(n_e):
        for dt in range(n_t):
            if de or dt:
                pl.semaphore_signal(
                    barrier,
                    inc=1,
                    device_id={"expert": lax.rem(me + de, n_e), "token": lax.rem(x + dt, n_t)},
                    device_id_type=MESH,
                )

    @pl.when(seg > 0)
    def _():
        pl.semaphore_signal(barrier, inc=1, device_id={"segment": seg - 1}, device_id_type=MESH)

    @pl.when(seg < n_seg - 1)
    def _():
        pl.semaphore_signal(barrier, inc=1, device_id={"segment": seg + 1}, device_id_type=MESH)

    inner = jnp.where(seg > 0, 1, 0) + jnp.where(seg < n_seg - 1, 1, 0)
    pl.semaphore_wait(barrier, n_e * n_t - 1 + inner)

    c0 = []
    c1 = []
    for s in range(3):
        c1.append(
            [
                go(
                    rcopy(
                        ins[s].at[0, :, cols(x)],
                        X.at[s, k, j0, :, cols(x)],
                        s1.at[s, d - 1],
                        r1.at[s, d - 1],
                        {"expert": lax.rem(j0 + d, J) * 2 + k},
                    )
                )
                for d in range(1, J)
            ]
        )
        c0.append(go(rcopy(ins[s].at[0], X.at[s, k, j0], s0.at[s], r0.at[s], {"expert": sib})))

    def normed_block(s, raw):
        wide = raw.astype(f32)
        inverse = lax.rsqrt(jnp.mean(wide * wide, axis=-1, keepdims=True) + norm_eps)
        scaled = wide * inverse
        return (scaled * gain[...]).astype(bf16), inverse

    lane = lax.broadcasted_iota(jnp.int32, (tok, E), 1)

    def gating(normed, first):
        logits = lax.dot_general(
            normed.astype(f32), router_t[...], NT, precision=highest, preferred_element_type=f32
        )
        probs = jax.nn.sigmoid(logits)
        picked = jnp.zeros((tok, E), f32)
        kept = jnp.zeros((tok, E), f32)
        for c in range(K):
            code = codes[:, first + c : first + c + 1]
            held = (code == lane).astype(f32)
            kept += held
            picked += held + (code == lane + E).astype(f32)
        total = jnp.sum(picked * probs, axis=-1, keepdims=True)
        return logits, probs, picked, kept, total, kept * (route_scale * probs / total)

    for c in local:
        c.wait()
    normed_a, _ = normed_block(0, X[0, k, j0])
    gates_a = gating(normed_a, 0)[5]
    normed_b, inverse_b = normed_block(1, X[1, k, j0])
    logits_b, probs_b, picked_b, kept_b, total_b, gates_b = gating(normed_b, K)
    own[0, :, 0:E] = logits_b
    own[1, :, 0:E] = probs_b
    own[2, :, 0:E] = picked_b
    own[3, :, 0:E] = kept_b
    own[4, :, 0:E] = jnp.broadcast_to(total_b, (tok, E))
    own[5, :, 0:E] = jnp.broadcast_to(inverse_b, (tok, E))
    G[k, j0] = jnp.zeros((tok, 128), f32)
    G[k, j0, :, 0:E] = gates_a
    G[k, j0, :, E : 2 * E] = gates_b
    cg = [
        go(
            rcopy(
                G.at[k, j0],
                G.at[k, j0],
                sg.at[d - 1],
                rg.at[d - 1],
                {"expert": lax.rem(me + d, n_e)},
            )
        )
        for d in range(1, n_e)
    ]

    def relay_first(s):
        out = []
        for d in range(1, J):
            src = lax.rem(j0 - d + J, J)
            c1[s][d - 1].wait_recv()
            part = X.at[s, k, src, :, cols(x)]
            to_tok = [
                go(
                    rcopy(
                        part,
                        part,
                        stok.at[s, d - 1, t - 1],
                        rtok.at[s, d - 1, t - 1],
                        {"token": lax.rem(x + t, n_t)},
                    )
                )
                for t in range(1, n_t)
            ]
            to_sib = go(
                rcopy(part, part, ssib.at[s, d - 1, 0], rsib.at[s, d - 1, 0], {"expert": sib})
            )
            out.append((to_tok, to_sib))
        return out

    def relay_second(s, first):
        sibs = []
        for d in range(1, J):
            src = lax.rem(j0 - d + J, J)
            to_tok, to_sib = first[d - 1]
            sibs.append(to_sib)
            for t in range(1, n_t):
                to_tok[t - 1].wait_recv()
                part = X.at[s, k, src, :, cols(lax.rem(x - t + n_t, n_t))]
                sibs.append(
                    go(
                        rcopy(
                            part, part, ssib.at[s, d - 1, t], rsib.at[s, d - 1, t], {"expert": sib}
                        )
                    )
                )
        return sibs

    def arrive(s, sibs):
        c0[s].wait_recv()
        for c in sibs:
            c.wait_recv()

    def normalize_all(s):
        def step(i, carry):
            p = i // J
            j = lax.rem(i, J)
            N[p, j] = normed_block(s, X[s, p, j])[0]
            return carry

        lax.fori_loop(0, n_e, step, 0)

    def column(s, e):
        want = s * E + me * per + e
        lanes = lax.broadcasted_iota(jnp.int32, (T, 128), 1)
        return jnp.sum(jnp.where(lanes == want, G[...].reshape(T, 128), 0.0), axis=1, keepdims=True)

    tile = min(512, W)

    def produce(r, emit):
        copies = []
        for ti in list(range(1, n_t)) + [0]:
            share = lax.rem(x + ti, n_t)

            def step(n, carry):
                at = pl.multiple_of(share * W + n * tile, tile)
                value = emit(at).astype(bf16).reshape(2, J, tok, tile)
                Pb[r, ti, :, :, :, pl.ds(pl.multiple_of(n * tile, tile), tile)] = value
                return carry

            lax.fori_loop(0, W // tile, step, 0)
            copies.append(
                go(
                    rcopy(
                        Pb.at[r, ti, 1 - k],
                        R1.at[r, ti],
                        sR1.at[r, ti],
                        rR1.at[r, ti],
                        {"expert": sib},
                    )
                )
            )
        return copies

    def pair_sum(r, ti):
        return Pb[r, ti, k].astype(f32) + R1[r, ti].astype(f32)

    def exchange(r, copies):
        sent = []
        for ti in range(1, n_t):
            copies[ti - 1].wait_recv()
            Q[r, ti - 1] = pair_sum(r, ti).astype(bf16)
            sent.append(
                go(
                    rcopy(
                        Q.at[r, ti - 1],
                        R2.at[r, ti - 1],
                        sR2.at[r, ti - 1],
                        rR2.at[r, ti - 1],
                        {"token": lax.rem(x + ti, n_t)},
                    )
                )
            )
        copies[n_t - 1].wait_recv()
        return sent

    def cross(r, sent):
        for c in sent:
            c.wait_recv()
        total = pair_sum(r, 0)
        for ti in range(1, n_t):
            total += R2[r, ti - 1].astype(f32)
        Z[r] = total.astype(bf16)
        return [
            go(
                rcopy(
                    Z.at[r, lax.rem(j0 + d, J)],
                    R3.at[r, d - 1],
                    sR3.at[r, d - 1],
                    rR3.at[r, d - 1],
                    {"expert": lax.rem(j0 + d, J) * 2 + k},
                )
            )
            for d in range(1, J)
        ]

    def gathered(r, sent):
        for c in sent:
            c.wait_recv()
        total = Z[r, j0].astype(f32)
        for d in range(1, J):
            total += R3[r, d - 1].astype(f32)
        return total

    first_a = relay_first(0)
    sibs_a = relay_second(0, first_a)
    arrive(0, sibs_a)
    normalize_all(0)
    weights[0].wait()
    weights[1].wait()
    for c in cg:
        c.wait_recv()

    first_b = relay_first(1)

    def fwd_step(e, carry):
        rows = N[...].reshape(T, D)
        gate = mm(rows, wg[e], NT)
        up = mm(rows, wu[e], NT)
        gg[e] = (gate * jax.nn.sigmoid(gate) * up * column(0, e)).astype(bf16)
        return carry

    lax.fori_loop(0, per, fwd_step, 0)
    weights[2].wait()
    first_c = relay_first(2)
    sibs_b = relay_second(1, first_b)

    def emit_fwd(at):
        total = mm(gg[0], wd[0, :, pl.ds(at, tile)])
        for e in range(1, per):
            total += mm(gg[e], wd[e, :, pl.ds(at, tile)])
        return total

    p_fwd = produce(0, emit_fwd)
    sibs_c = relay_second(2, first_c)
    sent_fwd = exchange(0, p_fwd)
    arrive(1, sibs_b)
    arrive(2, sibs_c)
    normalize_all(1)
    Sc[...] = jnp.zeros((T, 128), f32)

    def bwd_step(e, carry):
        rows = N[...].reshape(T, D)
        gate = mm(rows, wg[e], NT)
        up = mm(rows, wu[e], NT)
        grad_act = mm(X[2].reshape(T, D), wd[e], NT)
        sigma = jax.nn.sigmoid(gate)
        silu = gate * sigma
        ggv = grad_act * up * sigma * (1.0 + gate * (1.0 - sigma))
        guv = grad_act * silu
        col = column(1, e)
        dg = jnp.sum(guv * up, axis=1, keepdims=True)
        corr = col * jnp.sum(ggv * gate + guv * up, axis=1, keepdims=True)
        lanes = lax.broadcasted_iota(jnp.int32, (T, 128), 1)
        Sc[...] += jnp.where(lanes == e, dg, 0.0) + jnp.where(lanes == per, corr, 0.0)
        gg[e] = (ggv * col).astype(bf16)
        gu[e] = (guv * col).astype(bf16)
        return carry

    lax.fori_loop(0, per, bwd_step, 0)
    cross_fwd = cross(0, sent_fwd)

    flipped = jnp.transpose(Sc[...])[0:8]
    for p in range(2):
        for j in range(J):
            at = (p * J + j) * tok
            Sb[j * 2 + p] = flipped[:, at : at + tok]
    cs = []
    for de in range(n_e):
        for dt in range(n_t):
            if de or dt:
                to = lax.rem(me + de, n_e)
                cs.append(
                    go(
                        rcopy(
                            Sb.at[to],
                            RS.at[me, x],
                            sS.at[de, dt],
                            rS.at[de, dt],
                            {"expert": to, "token": lax.rem(x + dt, n_t)},
                        )
                    )
                )
    RS[me, x] = Sb[me]

    def emit_bwd(at):
        total = None
        for e in range(per):
            for grads, w in ((gg, wg), (gu, wu)):
                piece = mm(grads[e], w[e, :, pl.ds(at, tile)])
                total = piece if total is None else total + piece
        return total

    p_bwd = produce(1, emit_bwd)

    next_rows = X[0, k, j0, :, cols(x)].astype(f32) + gathered(0, cross_fwd)
    zbuf[0] = next_rows.astype(bf16)

    def send_next():
        return rcopy(
            zbuf.at[0], out_next.at[0], sz.at[0], rz.at[0], {"segment": lax.rem(seg + 1, n_seg)}
        )

    def send_prev():
        return rcopy(
            zbuf.at[1],
            out_prev.at[0],
            sz.at[1],
            rz.at[1],
            {"segment": lax.rem(seg - 1 + n_seg, n_seg)},
        )

    @pl.when(seg < n_seg - 1)
    def _():
        send_next().start()

    @pl.when(seg == 0)
    def _():
        out_next[...] = jnp.zeros(out_next.shape, bf16)

    @pl.when(seg == n_seg - 1)
    def _():
        out_prev[...] = jnp.zeros(out_prev.shape, bf16)

    sent_bwd = exchange(1, p_bwd)

    for c in cs:
        c.wait_recv()
    DGT[...] = jnp.zeros(DGT.shape, f32)
    corr = jnp.zeros((1, tok), f32)
    for e in range(n_e):
        total = RS[e, 0]
        for t in range(1, n_t):
            total += RS[e, t]
        DGT[e * per : (e + 1) * per, 0:tok] = total[0:per]
        corr += total[per : per + 1]
    DGT[E : E + 1, 0:tok] = corr
    turned = jnp.transpose(DGT[...])[0:tok]
    logits_b = own[0, :, 0:E]
    probs_b = own[1, :, 0:E]
    total_b = own[4, :, 0:E]
    inverse_b = own[5, :, 0:1]
    dgates = jnp.where(own[3, :, 0:E] > 0.5, turned[:, 0:E], 0.0)
    spread = jnp.sum(dgates * probs_b, axis=-1, keepdims=True)
    dprobs = route_scale * dgates / total_b - route_scale * spread / (total_b * total_b)
    dlogits = jnp.where(own[2, :, 0:E] > 0.5, dprobs * probs_b * (1.0 - probs_b), 0.0)
    mean_all = (turned[:, E : E + 1] + jnp.sum(dlogits * logits_b, axis=-1, keepdims=True)) / D
    router_own = lax.dot_general(
        dlogits, router_t[:, cols(x)], NN, precision=highest, preferred_element_type=f32
    )
    gain_own = gain[:, cols(x)]
    scaled_own = X[1, k, j0, :, cols(x)].astype(f32) * inverse_b
    cot_own = X[2, k, j0, :, cols(x)].astype(f32)
    base = cot_own + inverse_b * (router_own * gain_own - scaled_own * mean_all)

    cross_bwd = cross(1, sent_bwd)
    zbuf[1] = (base + inverse_b * gain_own * gathered(1, cross_bwd)).astype(bf16)

    @pl.when(seg > 0)
    def _():
        send_prev().start()

    for c in started:
        c.wait_send()

    @pl.when(seg < n_seg - 1)
    def _():
        send_next().wait_send()
        send_prev().wait_recv()

    @pl.when(seg > 0)
    def _():
        send_prev().wait_send()
        send_next().wait_recv()


def body(
    fwd_acts,
    fwd_ids,
    fwd_slots,
    bwd_acts,
    bwd_ids,
    bwd_slots,
    bwd_grad,
    norm_gain,
    router,
    w_gate,
    w_up,
    w_down,
):
    E = router.shape[2]
    per, D, F = w_gate.shape
    n_seg = lax.axis_size("segment")
    n_e = lax.axis_size("expert")
    n_t = lax.axis_size("token")
    tok = fwd_acts.shape[1]
    K = fwd_ids.shape[2]
    cap = max(2, min(3 * tok * K // (4 * E), tok - 1))
    W = D // n_t
    J = n_e // 2
    T = n_e * tok
    V = pltpu.VMEM
    dma = pltpu.SemaphoreType.DMA
    peers = max(J - 1, 1)
    toks = max(n_t - 1, 1)
    scratch = [
        V((3, 2, J, tok, D), bf16),
        V((2, J, tok, D), bf16),
        V((2, J, tok, 128), f32),
        V((per, F, D), bf16),
        V((per, F, D), bf16),
        V((per, F, D), bf16),
        V((per, T, F), bf16),
        V((per, T, F), bf16),
        V((2, n_t, 2, J, tok, W), bf16),
        V((2, n_t, J, tok, W), bf16),
        V((2, toks, J, tok, W), bf16),
        V((2, toks, J, tok, W), bf16),
        V((2, J, tok, W), bf16),
        V((2, peers, tok, W), bf16),
        V((T, 128), f32),
        V((n_e, 8, tok), f32),
        V((n_e, n_t, 8, tok), f32),
        V((128, 128), f32),
        V((6, tok, 128), f32),
        V((2, tok, W), bf16),
        dma((3,)),
        dma((3,)),
        dma((3,)),
        dma((3,)),
        dma((3, peers)),
        dma((3, peers)),
        dma((n_e - 1,)),
        dma((n_e - 1,)),
        dma((3, peers, n_t)),
        dma((3, peers, n_t)),
        dma((3, peers, toks)),
        dma((3, peers, toks)),
        dma((2, n_t)),
        dma((2, n_t)),
        dma((2, toks)),
        dma((2, toks)),
        dma((2, peers)),
        dma((2, peers)),
        dma((n_e, n_t)),
        dma((n_e, n_t)),
        dma((2,)),
        dma((2,)),
    ]
    codes = jnp.concatenate(
        [
            ids[0] + jnp.where(slots[0] < cap, 0, E)
            for ids, slots in ((fwd_ids, fwd_slots), (bwd_ids, bwd_slots))
        ],
        axis=1,
    )
    vm = pl.BlockSpec(memory_space=pltpu.VMEM)
    hbm = pl.BlockSpec(memory_space=pl.ANY)
    out = jax.ShapeDtypeStruct((1, tok, W), bf16)
    sizes = (n_seg, n_e, n_t, per, E, tok, D, F, K)
    return pl.pallas_call(
        functools.partial(kernel, sizes),
        out_shape=(out, out),
        in_specs=[hbm] * 3 + [vm] * 3 + [hbm] * 3,
        out_specs=(vm, vm),
        scratch_shapes=scratch,
        compiler_params=pltpu.CompilerParams(
            collective_id=0, has_side_effects=True, vmem_limit_bytes=63 * 1024 * 1024
        ),
        name="relay_moe",
    )(
        fwd_acts,
        bwd_acts,
        bwd_grad,
        codes,
        norm_gain,
        router[0].T,
        jnp.swapaxes(w_gate, 1, 2),
        jnp.swapaxes(w_up, 1, 2),
        w_down,
    )


def solution(mesh):
    return jax.shard_map(
        body,
        mesh=mesh,
        in_specs=(
            P("segment", "expert", None),
            P("segment", "expert", None),
            P("segment", "expert", None),
            P("segment", "expert", None),
            P("segment", "expert", None),
            P("segment", "expert", None),
            P("segment", "expert", None),
            P("segment", None),
            P("segment", None, None),
            P("expert", None, "token"),
            P("expert", None, "token"),
            P("expert", "token", None),
        ),
        out_specs=(P("segment", "expert", "token"), P("segment", "expert", "token")),
        check_vma=False,
    )
```

```python
import functools

import jax
import jax.numpy as jnp
from jax import lax
from jax.experimental import pallas as pl
from jax.experimental.pallas import tpu as pltpu
from jax.sharding import PartitionSpec as P

route_scale = 2.446
norm_eps = 1e-06
highest = lax.Precision.HIGHEST
MESH = pl.DeviceIdType.MESH
f32 = jnp.float32
bf16 = jnp.bfloat16
NT = (((1,), (1,)), ((), ()))
NN = (((1,), (0,)), ((), ()))


def mm(a, b, dims=NN):
    return lax.dot_general(a, b, dims, preferred_element_type=f32)


def kernel(
    sizes,
    fa,
    ba,
    bg,
    codes,
    gain,
    router_t,
    wg_h,
    wu_h,
    wd_h,
    out_next,
    out_prev,
    X,
    N,
    G,
    wg,
    wu,
    wd,
    act,
    gg,
    gu,
    Pb,
    R1,
    QA,
    R2A,
    ZA,
    R3A,
    QB,
    R2B,
    ZB,
    R3B,
    Sc,
    Sb,
    RS,
    DGT,
    own,
    own_base,
    zbuf,
    turn,
    w_sem,
    l_sem,
    s0,
    r0,
    s1,
    r1,
    sg,
    rg,
    ssib,
    rsib,
    stok,
    rtok,
    sR1,
    rR1,
    sR2A,
    rR2A,
    sR3A,
    rR3A,
    sR2B,
    rR2B,
    sR3B,
    rR3B,
    sS,
    rS,
    sz,
    rz,
):
    n_seg, n_e, n_t, per, E, tok, D, F, K = sizes
    J = n_e // 2
    W = D // n_t
    T = n_e * tok
    seg = lax.axis_index("segment")
    me = lax.axis_index("expert")
    x = lax.axis_index("token")
    k = lax.rem(me, 2)
    j0 = me // 2
    sib = j0 * 2 + 1 - k

    def cols(share):
        return pl.ds(pl.multiple_of(share * W, 128), W)

    def rcopy(src, dst, ss, rs, dev):
        return pltpu.make_async_remote_copy(
            src_ref=src, dst_ref=dst, send_sem=ss, recv_sem=rs, device_id=dev, device_id_type=MESH
        )

    started = []

    def go(copy):
        copy.start()
        started.append(copy)
        return copy

    ins = (fa, ba, bg)
    local = []
    for s in range(3):
        c = pltpu.make_async_copy(ins[s].at[0], X.at[s, k, j0], l_sem.at[s])
        c.start()
        local.append(c)
    weights = [[], [], []]
    pairs = [(i, e) for e in range(per) for i in (0, 1)] + [(2, e) for e in range(per)]
    for i, e in pairs:
        c = pltpu.make_async_copy(((wg_h, wu_h, wd_h)[i]).at[e], (wg, wu, wd)[i].at[e], w_sem.at[i, e])
        c.start()
        weights[i].append(c)

    barrier = pltpu.get_barrier_semaphore()
    for de in range(n_e):
        for dt in range(n_t):
            if de or dt:
                pl.semaphore_signal(
                    barrier,
                    inc=1,
                    device_id={"expert": lax.rem(me + de, n_e), "token": lax.rem(x + dt, n_t)},
                    device_id_type=MESH,
                )

    @pl.when(seg > 0)
    def _():
        pl.semaphore_signal(barrier, inc=1, device_id={"segment": seg - 1}, device_id_type=MESH)

    @pl.when(seg < n_seg - 1)
    def _():
        pl.semaphore_signal(barrier, inc=1, device_id={"segment": seg + 1}, device_id_type=MESH)

    inner = jnp.where(seg > 0, 1, 0) + jnp.where(seg < n_seg - 1, 1, 0)
    pl.semaphore_wait(barrier, n_e * n_t - 1 + inner)

    c0 = []
    c1 = []
    for s in range(3):
        c1.append(
            [
                go(
                    rcopy(
                        ins[s].at[0, :, cols(x)],
                        X.at[s, k, j0, :, cols(x)],
                        s1.at[s, d - 1],
                        r1.at[s, d - 1],
                        {"expert": lax.rem(j0 + d, J) * 2 + k},
                    )
                )
                for d in range(1, J)
            ]
        )
        c0.append(go(rcopy(ins[s].at[0], X.at[s, k, j0], s0.at[s], r0.at[s], {"expert": sib})))

    def normed_block(s, raw):
        wide = raw.astype(f32)
        inverse = lax.rsqrt(jnp.mean(wide * wide, axis=-1, keepdims=True) + norm_eps)
        scaled = wide * inverse
        return (scaled * gain[...]).astype(bf16), inverse

    lane = lax.broadcasted_iota(jnp.int32, (tok, E), 1)
    turn[...] = jnp.zeros((128, 128), f32)
    turn[0 : 2 * K, 0:tok] = codes[...].astype(f32)
    codes_f = jnp.transpose(turn[...])[0:tok].astype(jnp.int32)

    def gating(normed, first):
        logits = lax.dot_general(
            normed.astype(f32), router_t[...], NT, precision=highest, preferred_element_type=f32
        )
        probs = jax.nn.sigmoid(logits)
        picked = jnp.zeros((tok, E), f32)
        kept = jnp.zeros((tok, E), f32)
        for c in range(K):
            code = codes_f[:, first + c : first + c + 1]
            held = (code == lane).astype(f32)
            kept += held
            picked += held + (code == lane + E).astype(f32)
        total = jnp.sum(picked * probs, axis=-1, keepdims=True)
        return logits, probs, picked, kept, total, kept * (route_scale * probs / total)

    for c in local:
        c.wait()
    normed_a, _ = normed_block(0, X[0, k, j0])
    gates_a = gating(normed_a, 0)[5]
    normed_b, inverse_b = normed_block(1, X[1, k, j0])
    logits_b, probs_b, picked_b, kept_b, total_b, gates_b = gating(normed_b, K)
    own[0, :, 0:E] = logits_b
    own[1, :, 0:E] = probs_b
    own[2, :, 0:E] = picked_b
    own[3, :, 0:E] = kept_b
    own[4, :, 0:E] = jnp.broadcast_to(total_b, (tok, E))
    own[5, :, 0:E] = jnp.broadcast_to(inverse_b, (tok, E))
    G[k, j0] = jnp.zeros((tok, 128), f32)
    G[k, j0, :, 0:E] = gates_a
    G[k, j0, :, E : 2 * E] = gates_b
    cg = [
        go(
            rcopy(
                G.at[k, j0],
                G.at[k, j0],
                sg.at[d - 1],
                rg.at[d - 1],
                {"expert": lax.rem(me + d, n_e)},
            )
        )
        for d in range(1, n_e)
    ]

    def relay_first(s):
        out = []
        for d in range(1, J):
            src = lax.rem(j0 - d + J, J)
            c1[s][d - 1].wait_recv()
            part = X.at[s, k, src, :, cols(x)]
            to_tok = [
                go(
                    rcopy(
                        part,
                        part,
                        stok.at[s, d - 1, t - 1],
                        rtok.at[s, d - 1, t - 1],
                        {"token": lax.rem(x + t, n_t)},
                    )
                )
                for t in range(1, n_t)
            ]
            to_sib = go(
                rcopy(part, part, ssib.at[s, d - 1, 0], rsib.at[s, d - 1, 0], {"expert": sib})
            )
            out.append((to_tok, to_sib))
        return out

    def relay_second(s, first):
        sibs = []
        for d in range(1, J):
            src = lax.rem(j0 - d + J, J)
            to_tok, to_sib = first[d - 1]
            sibs.append(to_sib)
            for t in range(1, n_t):
                to_tok[t - 1].wait_recv()
                part = X.at[s, k, src, :, cols(lax.rem(x - t + n_t, n_t))]
                sibs.append(
                    go(
                        rcopy(
                            part, part, ssib.at[s, d - 1, t], rsib.at[s, d - 1, t], {"expert": sib}
                        )
                    )
                )
        return sibs

    def arrive(s, sibs):
        c0[s].wait_recv()
        for c in sibs:
            c.wait_recv()

    def normalize(s, j):
        for p in range(2):
            N[p, j] = normed_block(s, X[s, p, j])[0]

    M = 2 * tok
    wide_lane = lax.broadcasted_iota(jnp.int32, (M, 128), 1)

    def column(s, e, j):
        want = s * E + me * per + e
        picked = jnp.where(wide_lane == want, G[:, j].reshape(M, 128), 0.0)
        return jnp.sum(picked, axis=1, keepdims=True)

    def put(ref, e, j, value):
        ref[e, :, j] = value.astype(bf16).reshape(2, tok, F)

    def fwd_part(e, j):
        rows = N[:, j].reshape(M, D)
        gate = mm(rows, wg[e], NT)
        up = mm(rows, wu[e], NT)
        put(act, e, j, gate * jax.nn.sigmoid(gate) * up * column(0, e, j))

    def bwd_part(e, j):
        rows = N[:, j].reshape(M, D)
        gate = mm(rows, wg[e], NT)
        up = mm(rows, wu[e], NT)
        grad_act = mm(X[2, :, j].reshape(M, D), wd[e], NT)
        sigma = jax.nn.sigmoid(gate)
        silu = gate * sigma
        ggv = grad_act * up * sigma * (1.0 + gate * (1.0 - sigma))
        guv = grad_act * silu
        col = column(1, e, j)
        dg = jnp.sum(guv * up, axis=1, keepdims=True)
        corr = col * jnp.sum(ggv * gate + guv * up, axis=1, keepdims=True)
        both = jnp.where(wide_lane == e, dg, 0.0) + jnp.where(wide_lane == per, corr, 0.0)
        both = both.reshape(2, tok, 128)
        Sc[:, j] = both if e == 0 else Sc[:, j] + both
        put(gg, e, j, ggv * col)
        put(gu, e, j, guv * col)

    def others(fn):
        if J == 2:
            fn(1 - j0)
        elif J > 2:

            def step(d, carry):
                fn(lax.rem(j0 + d, J))
                return carry

            lax.fori_loop(1, J, step, 0)

    H = W // 2

    def produce(r, h, emit):
        def step(n, carry):
            ti = lax.rem(n + 1, n_t)
            at = pl.multiple_of(lax.rem(x + ti, n_t) * W + h * H, H)
            Pb[r, h, :, ti] = emit(at).astype(bf16).reshape(2, J, tok, H)
            return carry

        lax.fori_loop(0, n_t, step, 0)
        return go(
            rcopy(Pb.at[r, h, 1 - k], R1.at[r, h], sR1.at[r, h], rR1.at[r, h], {"expert": sib})
        )

    def token_first(r, copy):
        copy.wait_recv()
        sent = []
        for ti in range(1, n_t):
            QA[r, ti - 1] = (Pb[r, 0, k, ti].astype(f32) + R1[r, 0, ti].astype(f32)).astype(bf16)
            sent.append(
                go(
                    rcopy(
                        QA.at[r, ti - 1],
                        R2A.at[r, ti - 1],
                        sR2A.at[r, ti - 1],
                        rR2A.at[r, ti - 1],
                        {"token": lax.rem(x + ti, n_t)},
                    )
                )
            )
        return sent

    def expert_first(r, copy):
        copy.wait_recv()
        sent = []
        for d in range(1, J):
            jd = lax.rem(j0 + d, J)
            total = Pb[r, 1, k, :, jd].astype(f32) + R1[r, 1, :, jd].astype(f32)
            QB[r, d - 1] = total.astype(bf16)
            sent.append(
                go(
                    rcopy(
                        QB.at[r, d - 1],
                        R2B.at[r, d - 1],
                        sR2B.at[r, d - 1],
                        rR2B.at[r, d - 1],
                        {"expert": jd * 2 + k},
                    )
                )
            )
        return sent

    def then_expert(r, sent):
        for c in sent:
            c.wait_recv()
        total = Pb[r, 0, k, 0].astype(f32) + R1[r, 0, 0].astype(f32)
        for ti in range(1, n_t):
            total += R2A[r, ti - 1].astype(f32)
        ZA[r] = total.astype(bf16)
        return [
            go(
                rcopy(
                    ZA.at[r, lax.rem(j0 + d, J)],
                    R3A.at[r, d - 1],
                    sR3A.at[r, d - 1],
                    rR3A.at[r, d - 1],
                    {"expert": lax.rem(j0 + d, J) * 2 + k},
                )
            )
            for d in range(1, J)
        ]

    def then_token(r, sent):
        for c in sent:
            c.wait_recv()
        total = Pb[r, 1, k, :, j0].astype(f32) + R1[r, 1, :, j0].astype(f32)
        for d in range(1, J):
            total += R2B[r, d - 1].astype(f32)
        ZB[r] = total.astype(bf16)
        return [
            go(
                rcopy(
                    ZB.at[r, ti],
                    R3B.at[r, ti - 1],
                    sR3B.at[r, ti - 1],
                    rR3B.at[r, ti - 1],
                    {"token": lax.rem(x + ti, n_t)},
                )
            )
            for ti in range(1, n_t)
        ]

    def last_a(r, sent):
        for c in sent:
            c.wait_recv()
        total = ZA[r, j0].astype(f32)
        for d in range(1, J):
            total += R3A[r, d - 1].astype(f32)
        return total

    def last_b(r, sent):
        for c in sent:
            c.wait_recv()
        total = ZB[r, 0].astype(f32)
        for ti in range(1, n_t):
            total += R3B[r, ti - 1].astype(f32)
        return total

    def half_cols(h):
        return pl.ds(pl.multiple_of(x * W + h * H, 128), H)

    def send_next(h):
        part = (0, slice(None), pl.ds(h * H, H))
        return rcopy(
            zbuf.at[part],
            out_next.at[part],
            sz.at[0, h],
            rz.at[0, h],
            {"segment": lax.rem(seg + 1, n_seg)},
        )

    def send_prev(h):
        part = (slice(None), pl.ds(h * H, H))
        return rcopy(
            zbuf.at[(1,) + part],
            out_prev.at[(0,) + part],
            sz.at[1, h],
            rz.at[1, h],
            {"segment": lax.rem(seg - 1 + n_seg, n_seg)},
        )

    def emit_fwd(at):
        total = None
        for e in range(per):
            piece = mm(act[e].reshape(T, F), wd[e, :, pl.ds(at, H)])
            total = piece if total is None else total + piece
        return total

    def emit_bwd(at):
        total = None
        for e in range(per):
            for grads, w in ((gg, wg), (gu, wu)):
                piece = mm(grads[e].reshape(T, F), w[e, :, pl.ds(at, H)])
                total = piece if total is None else total + piece
        return total

    def finish_next(h, mixed):
        rows = X[0, k, j0, :, half_cols(h)].astype(f32) + mixed
        zbuf[0, :, h * H : (h + 1) * H] = rows.astype(bf16)

        @pl.when(seg < n_seg - 1)
        def _():
            send_next(h).start()

    c0[0].wait_recv()
    normalize(0, j0)
    for c in cg:
        c.wait_recv()
    for e in range(per):
        weights[0][e].wait()
        weights[1][e].wait()
        fwd_part(e, j0)
        if e == 0:
            first_a = relay_first(0)
    c0[1].wait_recv()
    c0[2].wait_recv()
    normalize(1, j0)
    for e in range(per):
        weights[2][e].wait()
        bwd_part(e, j0)
        if e == 0:
            first_b = relay_first(1)
    sibs_a = relay_second(0, first_a)
    for c in sibs_a:
        c.wait_recv()
    others(lambda j: normalize(0, j))
    others(lambda j: fwd_part(0, j))
    first_c = relay_first(2)
    sibs_b = relay_second(1, first_b)
    for e in range(1, per):
        others(functools.partial(fwd_part, e))
    fa_copy = produce(0, 0, emit_fwd)
    sibs_c = relay_second(2, first_c)
    fb_copy = produce(0, 1, emit_fwd)
    for c in sibs_b:
        c.wait_recv()
    others(lambda j: normalize(1, j))
    for c in sibs_c:
        c.wait_recv()
    fa_sent = token_first(0, fa_copy)
    fb_sent = expert_first(0, fb_copy)
    for e in range(per):
        others(functools.partial(bwd_part, e))

    flipped = jnp.transpose(Sc[...].reshape(T, 128))[0:8]
    for p in range(2):
        for j in range(J):
            at = (p * J + j) * tok
            Sb[j * 2 + p] = flipped[:, at : at + tok]
    cs = []
    for de in range(n_e):
        for dt in range(n_t):
            if de or dt:
                to = lax.rem(me + de, n_e)
                cs.append(
                    go(
                        rcopy(
                            Sb.at[to],
                            RS.at[me, x],
                            sS.at[de, dt],
                            rS.at[de, dt],
                            {"expert": to, "token": lax.rem(x + dt, n_t)},
                        )
                    )
                )
    RS[me, x] = Sb[me]

    fa_sent = then_expert(0, fa_sent)
    fb_sent = then_token(0, fb_sent)
    ba_copy = produce(1, 0, emit_bwd)
    finish_next(0, last_a(0, fa_sent))
    finish_next(1, last_b(0, fb_sent))
    bb_copy = produce(1, 1, emit_bwd)
    ba_sent = token_first(1, ba_copy)
    bb_sent = expert_first(1, bb_copy)

    @pl.when(seg == 0)
    def _():
        out_next[...] = jnp.zeros(out_next.shape, bf16)

    @pl.when(seg == n_seg - 1)
    def _():
        out_prev[...] = jnp.zeros(out_prev.shape, bf16)

    for c in cs:
        c.wait_recv()
    DGT[...] = jnp.zeros(DGT.shape, f32)
    corr = jnp.zeros((1, tok), f32)
    for e in range(n_e):
        total = RS[e, 0]
        for t in range(1, n_t):
            total += RS[e, t]
        DGT[e * per : (e + 1) * per, 0:tok] = total[0:per]
        corr += total[per : per + 1]
    DGT[E : E + 1, 0:tok] = corr
    turned = jnp.transpose(DGT[...])[0:tok]
    logits_b = own[0, :, 0:E]
    probs_b = own[1, :, 0:E]
    total_b = own[4, :, 0:E]
    inverse_b = own[5, :, 0:1]
    dgates = jnp.where(own[3, :, 0:E] > 0.5, turned[:, 0:E], 0.0)
    spread = jnp.sum(dgates * probs_b, axis=-1, keepdims=True)
    dprobs = route_scale * dgates / total_b - route_scale * spread / (total_b * total_b)
    dlogits = jnp.where(own[2, :, 0:E] > 0.5, dprobs * probs_b * (1.0 - probs_b), 0.0)
    mean_all = (turned[:, E : E + 1] + jnp.sum(dlogits * logits_b, axis=-1, keepdims=True)) / D
    router_own = lax.dot_general(
        dlogits, router_t[:, cols(x)], NN, precision=highest, preferred_element_type=f32
    )
    gain_own = gain[:, cols(x)]
    scaled_own = X[1, k, j0, :, cols(x)].astype(f32) * inverse_b
    cot_own = X[2, k, j0, :, cols(x)].astype(f32)
    base = cot_own + inverse_b * (router_own * gain_own - scaled_own * mean_all)

    scale_own = inverse_b * gain_own
    own_base[...] = base
    ba_sent = then_expert(1, ba_sent)
    bb_sent = then_token(1, bb_sent)

    def finish_prev(h, mixed):
        at = slice(h * H, (h + 1) * H)
        zbuf[1, :, at] = (own_base[:, at] + scale_own[:, at] * mixed).astype(bf16)

        @pl.when(seg > 0)
        def _():
            send_prev(h).start()

    finish_prev(0, last_a(1, ba_sent))
    finish_prev(1, last_b(1, bb_sent))

    for c in started:
        c.wait_send()

    @pl.when(seg < n_seg - 1)
    def _():
        for h in range(2):
            send_next(h).wait_send()
            send_prev(h).wait_recv()

    @pl.when(seg > 0)
    def _():
        for h in range(2):
            send_prev(h).wait_send()
            send_next(h).wait_recv()


def settle(next_in, prev_in, next_out, prev_out):
    next_out[...] = next_in[...]
    prev_out[...] = prev_in[...]


def body(
    fwd_acts,
    fwd_ids,
    fwd_slots,
    bwd_acts,
    bwd_ids,
    bwd_slots,
    bwd_grad,
    norm_gain,
    router,
    w_gate,
    w_up,
    w_down,
):
    E = router.shape[2]
    per, D, F = w_gate.shape
    n_seg = lax.axis_size("segment")
    n_e = lax.axis_size("expert")
    n_t = lax.axis_size("token")
    tok = fwd_acts.shape[1]
    K = fwd_ids.shape[2]
    cap = max(2, min(3 * tok * K // (4 * E), tok - 1))
    W = D // n_t
    J = n_e // 2
    T = n_e * tok
    V = pltpu.VMEM
    dma = pltpu.SemaphoreType.DMA
    peers = max(J - 1, 1)
    toks = max(n_t - 1, 1)
    scratch = [
        V((3, 2, J, tok, D), bf16),
        V((2, J, tok, D), bf16),
        V((2, J, tok, 128), f32),
        V((per, F, D), bf16),
        V((per, F, D), bf16),
        V((per, F, D), bf16),
        V((per, 2, J, tok, F), bf16),
        V((per, 2, J, tok, F), bf16),
        V((per, 2, J, tok, F), bf16),
        V((2, 2, 2, n_t, J, tok, W // 2), bf16),
        V((2, 2, n_t, J, tok, W // 2), bf16),
        V((2, toks, J, tok, W // 2), bf16),
        V((2, toks, J, tok, W // 2), bf16),
        V((2, J, tok, W // 2), bf16),
        V((2, peers, tok, W // 2), bf16),
        V((2, peers, n_t, tok, W // 2), bf16),
        V((2, peers, n_t, tok, W // 2), bf16),
        V((2, n_t, tok, W // 2), bf16),
        V((2, toks, tok, W // 2), bf16),
        V((2, J, tok, 128), f32),
        V((n_e, 8, tok), f32),
        V((n_e, n_t, 8, tok), f32),
        V((128, 128), f32),
        V((6, tok, 128), f32),
        V((tok, W), f32),
        V((2, tok, W), bf16),
        V((128, 128), f32),
        dma((3, per)),
        dma((3,)),
        dma((3,)),
        dma((3,)),
        dma((3, peers)),
        dma((3, peers)),
        dma((n_e - 1,)),
        dma((n_e - 1,)),
        dma((3, peers, n_t)),
        dma((3, peers, n_t)),
        dma((3, peers, toks)),
        dma((3, peers, toks)),
        dma((2, 2)),
        dma((2, 2)),
        dma((2, toks)),
        dma((2, toks)),
        dma((2, peers)),
        dma((2, peers)),
        dma((2, peers)),
        dma((2, peers)),
        dma((2, toks)),
        dma((2, toks)),
        dma((n_e, n_t)),
        dma((n_e, n_t)),
        dma((2, 2)),
        dma((2, 2)),
    ]
    codes = jnp.concatenate(
        [
            (ids[0] + jnp.where(slots[0] < cap, 0, E)).T
            for ids, slots in ((fwd_ids, fwd_slots), (bwd_ids, bwd_slots))
        ],
        axis=0,
    )
    vm = pl.BlockSpec(memory_space=pltpu.VMEM)
    hbm = pl.BlockSpec(memory_space=pl.ANY)
    out = jax.ShapeDtypeStruct((1, tok, W), bf16)
    sizes = (n_seg, n_e, n_t, per, E, tok, D, F, K)
    moved = pl.pallas_call(
        functools.partial(kernel, sizes),
        out_shape=(out, out),
        in_specs=[hbm] * 3 + [vm] * 3 + [hbm] * 3,
        out_specs=(vm, vm),
        scratch_shapes=scratch,
        compiler_params=pltpu.CompilerParams(
            collective_id=0, has_side_effects=True, vmem_limit_bytes=63 * 1024 * 1024
        ),
        name="relay_moe",
    )(
        fwd_acts,
        bwd_acts,
        bwd_grad,
        codes,
        norm_gain,
        router[0].T,
        jnp.swapaxes(w_gate, 1, 2),
        jnp.swapaxes(w_up, 1, 2),
        w_down,
    )
    return pl.pallas_call(
        settle, out_shape=(out, out), in_specs=[vm] * 2, out_specs=(vm, vm), name="settle"
    )(*moved)


def solution(mesh):
    return jax.shard_map(
        body,
        mesh=mesh,
        in_specs=(
            P("segment", "expert", None),
            P("segment", "expert", None),
            P("segment", "expert", None),
            P("segment", "expert", None),
            P("segment", "expert", None),
            P("segment", "expert", None),
            P("segment", "expert", None),
            P("segment", None),
            P("segment", None, None),
            P("expert", None, "token"),
            P("expert", None, "token"),
            P("expert", "token", None),
        ),
        out_specs=(P("segment", "expert", "token"), P("segment", "expert", "token")),
        check_vma=False,
    )
```

```python
import functools

import jax
import jax.numpy as jnp
from jax import lax
from jax.experimental import pallas as pl
from jax.experimental.pallas import tpu as pltpu
from jax.sharding import PartitionSpec as P

route_scale = 2.446
norm_eps = 1e-06
highest = lax.Precision.HIGHEST
MESH = pl.DeviceIdType.MESH
f32 = jnp.float32
bf16 = jnp.bfloat16
NT = (((1,), (1,)), ((), ()))
NN = (((1,), (0,)), ((), ()))


def mm(a, b, dims=NN):
    return lax.dot_general(a, b, dims, preferred_element_type=f32)


def kernel(
    sizes,
    fa,
    ba,
    bg,
    codes,
    gain,
    router_t,
    wg_h,
    wu_h,
    wd_h,
    out_next,
    out_prev,
    X,
    N,
    G,
    wg,
    wu,
    wd,
    act,
    gg,
    gu,
    Pb,
    R1,
    QA,
    R2A,
    ZA,
    R3A,
    QB,
    R2B,
    ZB,
    R3B,
    Sc,
    Sb,
    RS,
    DGT,
    own,
    own_base,
    zbuf,
    turn,
    w_sem,
    l_sem,
    s0,
    r0,
    s1,
    r1,
    sg,
    rg,
    ssib,
    rsib,
    stok,
    rtok,
    sR1,
    rR1,
    sR2A,
    rR2A,
    sR3A,
    rR3A,
    sR2B,
    rR2B,
    sR3B,
    rR3B,
    sS,
    rS,
    sz,
    rz,
):
    n_seg, n_e, n_t, per, E, tok, D, F, K = sizes
    J = n_e // 2
    W = D // n_t
    T = n_e * tok
    seg = lax.axis_index("segment")
    me = lax.axis_index("expert")
    x = lax.axis_index("token")
    k = lax.rem(me, 2)
    j0 = me // 2
    sib = j0 * 2 + 1 - k

    def cols(share):
        return pl.ds(pl.multiple_of(share * W, 128), W)

    def rcopy(src, dst, ss, rs, dev):
        return pltpu.make_async_remote_copy(
            src_ref=src, dst_ref=dst, send_sem=ss, recv_sem=rs, device_id=dev, device_id_type=MESH
        )

    started = []

    def go(copy):
        copy.start()
        started.append(copy)
        return copy

    ins = (fa, ba, bg)
    local = []
    for s in range(3):
        c = pltpu.make_async_copy(ins[s].at[0], X.at[s, k, j0], l_sem.at[s])
        c.start()
        local.append(c)
    weights = [[], [], []]
    pairs = [(i, e) for e in range(per) for i in (0, 1)] + [(2, e) for e in range(per)]
    for i, e in pairs:
        c = pltpu.make_async_copy(((wg_h, wu_h, wd_h)[i]).at[e], (wg, wu, wd)[i].at[e], w_sem.at[i, e])
        c.start()
        weights[i].append(c)

    barrier = pltpu.get_barrier_semaphore()
    for de in range(n_e):
        for dt in range(n_t):
            if de or dt:
                pl.semaphore_signal(
                    barrier,
                    inc=1,
                    device_id={"expert": lax.rem(me + de, n_e), "token": lax.rem(x + dt, n_t)},
                    device_id_type=MESH,
                )

    @pl.when(seg > 0)
    def _():
        pl.semaphore_signal(barrier, inc=1, device_id={"segment": seg - 1}, device_id_type=MESH)

    @pl.when(seg < n_seg - 1)
    def _():
        pl.semaphore_signal(barrier, inc=1, device_id={"segment": seg + 1}, device_id_type=MESH)

    inner = jnp.where(seg > 0, 1, 0) + jnp.where(seg < n_seg - 1, 1, 0)
    pl.semaphore_wait(barrier, n_e * n_t - 1 + inner)

    c0 = []
    c1 = []
    for s in range(3):
        c1.append(
            [
                go(
                    rcopy(
                        ins[s].at[0, :, cols(x)],
                        X.at[s, k, j0, :, cols(x)],
                        s1.at[s, d - 1],
                        r1.at[s, d - 1],
                        {"expert": lax.rem(j0 + d, J) * 2 + k},
                    )
                )
                for d in range(1, J)
            ]
        )
        c0.append(go(rcopy(ins[s].at[0], X.at[s, k, j0], s0.at[s], r0.at[s], {"expert": sib})))

    def normed_block(s, raw):
        wide = raw.astype(f32)
        inverse = lax.rsqrt(jnp.mean(wide * wide, axis=-1, keepdims=True) + norm_eps)
        scaled = wide * inverse
        return (scaled * gain[...]).astype(bf16), inverse

    lane = lax.broadcasted_iota(jnp.int32, (tok, E), 1)
    turn[...] = jnp.zeros((128, 128), f32)
    turn[0 : 2 * K, 0:tok] = codes[...].astype(f32)
    codes_f = jnp.transpose(turn[...])[0:tok].astype(jnp.int32)

    def gating(normed, first):
        logits = lax.dot_general(
            normed.astype(f32), router_t[...], NT, precision=highest, preferred_element_type=f32
        )
        probs = jax.nn.sigmoid(logits)
        picked = jnp.zeros((tok, E), f32)
        kept = jnp.zeros((tok, E), f32)
        for c in range(K):
            code = codes_f[:, first + c : first + c + 1]
            held = (code == lane).astype(f32)
            kept += held
            picked += held + (code == lane + E).astype(f32)
        total = jnp.sum(picked * probs, axis=-1, keepdims=True)
        return logits, probs, picked, kept, total, kept * (route_scale * probs / total)

    for c in local:
        c.wait()
    normed_a, _ = normed_block(0, X[0, k, j0])
    gates_a = gating(normed_a, 0)[5]
    normed_b, inverse_b = normed_block(1, X[1, k, j0])
    logits_b, probs_b, picked_b, kept_b, total_b, gates_b = gating(normed_b, K)
    own[0, :, 0:E] = logits_b
    own[1, :, 0:E] = probs_b
    own[2, :, 0:E] = picked_b
    own[3, :, 0:E] = kept_b
    own[4, :, 0:E] = jnp.broadcast_to(total_b, (tok, E))
    own[5, :, 0:E] = jnp.broadcast_to(inverse_b, (tok, E))
    G[k, j0] = jnp.zeros((tok, 128), f32)
    G[k, j0, :, 0:E] = gates_a
    G[k, j0, :, E : 2 * E] = gates_b
    cg = [
        go(
            rcopy(
                G.at[k, j0],
                G.at[k, j0],
                sg.at[d - 1],
                rg.at[d - 1],
                {"expert": lax.rem(me + d, n_e)},
            )
        )
        for d in range(1, n_e)
    ]

    def relay_first(s):
        out = []
        for d in range(1, J):
            src = lax.rem(j0 - d + J, J)
            c1[s][d - 1].wait_recv()
            part = X.at[s, k, src, :, cols(x)]
            to_tok = [
                go(
                    rcopy(
                        part,
                        part,
                        stok.at[s, d - 1, t - 1],
                        rtok.at[s, d - 1, t - 1],
                        {"token": lax.rem(x + t, n_t)},
                    )
                )
                for t in range(1, n_t)
            ]
            to_sib = go(
                rcopy(part, part, ssib.at[s, d - 1, 0], rsib.at[s, d - 1, 0], {"expert": sib})
            )
            out.append((to_tok, to_sib))
        return out

    def relay_second(s, first):
        sibs = []
        for d in range(1, J):
            src = lax.rem(j0 - d + J, J)
            to_tok, to_sib = first[d - 1]
            sibs.append(to_sib)
            for t in range(1, n_t):
                to_tok[t - 1].wait_recv()
                part = X.at[s, k, src, :, cols(lax.rem(x - t + n_t, n_t))]
                sibs.append(
                    go(
                        rcopy(
                            part, part, ssib.at[s, d - 1, t], rsib.at[s, d - 1, t], {"expert": sib}
                        )
                    )
                )
        return sibs

    def arrive(s, sibs):
        c0[s].wait_recv()
        for c in sibs:
            c.wait_recv()

    def normalize(s, j):
        for p in range(2):
            N[p, j] = normed_block(s, X[s, p, j])[0]

    M = T
    wide_lane = lax.broadcasted_iota(jnp.int32, (M, 128), 1)

    def column(s, e):
        want = s * E + me * per + e
        picked = jnp.where(wide_lane == want, G[...].reshape(M, 128), 0.0)
        return jnp.sum(picked, axis=1, keepdims=True)

    def put(ref, e, value):
        ref[e] = value.astype(bf16)

    def fwd_part(e):
        rows = N[...].reshape(M, D)
        gate = mm(rows, wg[e], NT)
        up = mm(rows, wu[e], NT)
        put(act, e, gate * jax.nn.sigmoid(gate) * up * column(0, e))

    def bwd_part(e):
        rows = N[...].reshape(M, D)
        gate = mm(rows, wg[e], NT)
        up = mm(rows, wu[e], NT)
        grad_act = mm(X[2].reshape(M, D), wd[e], NT)
        sigma = jax.nn.sigmoid(gate)
        silu = gate * sigma
        ggv = grad_act * up * sigma * (1.0 + gate * (1.0 - sigma))
        guv = grad_act * silu
        col = column(1, e)
        dg = jnp.sum(guv * up, axis=1, keepdims=True)
        corr = col * jnp.sum(ggv * gate + guv * up, axis=1, keepdims=True)
        both = jnp.where(wide_lane == e, dg, 0.0) + jnp.where(wide_lane == per, corr, 0.0)
        Sc[...] = both if e == 0 else Sc[...] + both
        put(gg, e, ggv * col)
        put(gu, e, guv * col)

    def others(fn):
        if J == 2:
            fn(1 - j0)
        elif J > 2:

            def step(d, carry):
                fn(lax.rem(j0 + d, J))
                return carry

            lax.fori_loop(1, J, step, 0)

    H = W // 2

    def produce(r, h, emit):
        def step(n, carry):
            ti = lax.rem(n + 1, n_t)
            at = pl.multiple_of(lax.rem(x + ti, n_t) * W + h * H, H)
            Pb[r, h, :, ti] = emit(at).astype(bf16).reshape(2, J, tok, H)
            return carry

        lax.fori_loop(0, n_t, step, 0)
        return go(
            rcopy(Pb.at[r, h, 1 - k], R1.at[r, h], sR1.at[r, h], rR1.at[r, h], {"expert": sib})
        )

    def token_first(r, copy):
        copy.wait_recv()
        sent = []
        for ti in range(1, n_t):
            QA[r, ti - 1] = (Pb[r, 0, k, ti].astype(f32) + R1[r, 0, ti].astype(f32)).astype(bf16)
            sent.append(
                go(
                    rcopy(
                        QA.at[r, ti - 1],
                        R2A.at[r, ti - 1],
                        sR2A.at[r, ti - 1],
                        rR2A.at[r, ti - 1],
                        {"token": lax.rem(x + ti, n_t)},
                    )
                )
            )
        return sent

    def expert_first(r, copy):
        copy.wait_recv()
        sent = []
        for d in range(1, J):
            jd = lax.rem(j0 + d, J)
            total = Pb[r, 1, k, :, jd].astype(f32) + R1[r, 1, :, jd].astype(f32)
            QB[r, d - 1] = total.astype(bf16)
            sent.append(
                go(
                    rcopy(
                        QB.at[r, d - 1],
                        R2B.at[r, d - 1],
                        sR2B.at[r, d - 1],
                        rR2B.at[r, d - 1],
                        {"expert": jd * 2 + k},
                    )
                )
            )
        return sent

    def then_expert(r, sent):
        for c in sent:
            c.wait_recv()
        total = Pb[r, 0, k, 0].astype(f32) + R1[r, 0, 0].astype(f32)
        for ti in range(1, n_t):
            total += R2A[r, ti - 1].astype(f32)
        ZA[r] = total.astype(bf16)
        return [
            go(
                rcopy(
                    ZA.at[r, lax.rem(j0 + d, J)],
                    R3A.at[r, d - 1],
                    sR3A.at[r, d - 1],
                    rR3A.at[r, d - 1],
                    {"expert": lax.rem(j0 + d, J) * 2 + k},
                )
            )
            for d in range(1, J)
        ]

    def then_token(r, sent):
        for c in sent:
            c.wait_recv()
        total = Pb[r, 1, k, :, j0].astype(f32) + R1[r, 1, :, j0].astype(f32)
        for d in range(1, J):
            total += R2B[r, d - 1].astype(f32)
        ZB[r] = total.astype(bf16)
        return [
            go(
                rcopy(
                    ZB.at[r, ti],
                    R3B.at[r, ti - 1],
                    sR3B.at[r, ti - 1],
                    rR3B.at[r, ti - 1],
                    {"token": lax.rem(x + ti, n_t)},
                )
            )
            for ti in range(1, n_t)
        ]

    def last_a(r, sent):
        for c in sent:
            c.wait_recv()
        total = ZA[r, j0].astype(f32)
        for d in range(1, J):
            total += R3A[r, d - 1].astype(f32)
        return total

    def last_b(r, sent):
        for c in sent:
            c.wait_recv()
        total = ZB[r, 0].astype(f32)
        for ti in range(1, n_t):
            total += R3B[r, ti - 1].astype(f32)
        return total

    def half_cols(h):
        return pl.ds(pl.multiple_of(x * W + h * H, 128), H)

    def send_next(h):
        part = (0, slice(None), pl.ds(h * H, H))
        return rcopy(
            zbuf.at[part],
            out_next.at[part],
            sz.at[0, h],
            rz.at[0, h],
            {"segment": lax.rem(seg + 1, n_seg)},
        )

    def send_prev(h):
        part = (slice(None), pl.ds(h * H, H))
        return rcopy(
            zbuf.at[(1,) + part],
            out_prev.at[(0,) + part],
            sz.at[1, h],
            rz.at[1, h],
            {"segment": lax.rem(seg - 1 + n_seg, n_seg)},
        )

    def emit_fwd(at):
        total = None
        for e in range(per):
            piece = mm(act[e], wd[e, :, pl.ds(at, H)])
            total = piece if total is None else total + piece
        return total

    def emit_bwd(at):
        total = None
        for e in range(per):
            for grads, w in ((gg, wg), (gu, wu)):
                piece = mm(grads[e], w[e, :, pl.ds(at, H)])
                total = piece if total is None else total + piece
        return total

    def finish_next(h, mixed):
        rows = X[0, k, j0, :, half_cols(h)].astype(f32) + mixed
        zbuf[0, :, h * H : (h + 1) * H] = rows.astype(bf16)

        @pl.when(seg < n_seg - 1)
        def _():
            send_next(h).start()

    c0[0].wait_recv()
    normalize(0, j0)
    first_a = relay_first(0)
    for c in cg:
        c.wait_recv()
    first_b = relay_first(1)
    for c in relay_second(0, first_a):
        c.wait_recv()
    others(lambda j: normalize(0, j))
    for e in range(per):
        weights[0][e].wait()
        weights[1][e].wait()
        fwd_part(e)
        if e == 0:
            first_c = relay_first(2)
            sibs_b = relay_second(1, first_b)
    c0[1].wait_recv()
    c0[2].wait_recv()
    for e in range(per):
        weights[2][e].wait()
    fa_copy = produce(0, 0, emit_fwd)
    sibs_c = relay_second(2, first_c)
    fb_copy = produce(0, 1, emit_fwd)
    for c in sibs_b:
        c.wait_recv()
    normalize(1, j0)
    others(lambda j: normalize(1, j))
    for c in sibs_c:
        c.wait_recv()
    fa_sent = token_first(0, fa_copy)
    fb_sent = expert_first(0, fb_copy)
    for e in range(per):
        bwd_part(e)

    flipped = jnp.transpose(Sc[...])[0:8]
    for p in range(2):
        for j in range(J):
            at = (p * J + j) * tok
            Sb[j * 2 + p] = flipped[:, at : at + tok]
    cs = []
    for de in range(n_e):
        for dt in range(n_t):
            if de or dt:
                to = lax.rem(me + de, n_e)
                cs.append(
                    go(
                        rcopy(
                            Sb.at[to],
                            RS.at[me, x],
                            sS.at[de, dt],
                            rS.at[de, dt],
                            {"expert": to, "token": lax.rem(x + dt, n_t)},
                        )
                    )
                )
    RS[me, x] = Sb[me]

    fa_sent = then_expert(0, fa_sent)
    fb_sent = then_token(0, fb_sent)
    ba_copy = produce(1, 0, emit_bwd)
    finish_next(0, last_a(0, fa_sent))
    finish_next(1, last_b(0, fb_sent))
    bb_copy = produce(1, 1, emit_bwd)
    ba_sent = token_first(1, ba_copy)
    bb_sent = expert_first(1, bb_copy)

    @pl.when(seg == 0)
    def _():
        out_next[...] = jnp.zeros(out_next.shape, bf16)

    @pl.when(seg == n_seg - 1)
    def _():
        out_prev[...] = jnp.zeros(out_prev.shape, bf16)

    for c in cs:
        c.wait_recv()
    DGT[...] = jnp.zeros(DGT.shape, f32)
    corr = jnp.zeros((1, tok), f32)
    for e in range(n_e):
        total = RS[e, 0]
        for t in range(1, n_t):
            total += RS[e, t]
        DGT[e * per : (e + 1) * per, 0:tok] = total[0:per]
        corr += total[per : per + 1]
    DGT[E : E + 1, 0:tok] = corr
    turned = jnp.transpose(DGT[...])[0:tok]
    logits_b = own[0, :, 0:E]
    probs_b = own[1, :, 0:E]
    total_b = own[4, :, 0:E]
    inverse_b = own[5, :, 0:1]
    dgates = jnp.where(own[3, :, 0:E] > 0.5, turned[:, 0:E], 0.0)
    spread = jnp.sum(dgates * probs_b, axis=-1, keepdims=True)
    dprobs = route_scale * dgates / total_b - route_scale * spread / (total_b * total_b)
    dlogits = jnp.where(own[2, :, 0:E] > 0.5, dprobs * probs_b * (1.0 - probs_b), 0.0)
    mean_all = (turned[:, E : E + 1] + jnp.sum(dlogits * logits_b, axis=-1, keepdims=True)) / D
    router_own = lax.dot_general(
        dlogits, router_t[:, cols(x)], NN, precision=highest, preferred_element_type=f32
    )
    gain_own = gain[:, cols(x)]
    scaled_own = X[1, k, j0, :, cols(x)].astype(f32) * inverse_b
    cot_own = X[2, k, j0, :, cols(x)].astype(f32)
    base = cot_own + inverse_b * (router_own * gain_own - scaled_own * mean_all)

    scale_own = inverse_b * gain_own
    own_base[...] = base
    ba_sent = then_expert(1, ba_sent)
    bb_sent = then_token(1, bb_sent)

    def finish_prev(h, mixed):
        at = slice(h * H, (h + 1) * H)
        zbuf[1, :, at] = (own_base[:, at] + scale_own[:, at] * mixed).astype(bf16)

        @pl.when(seg > 0)
        def _():
            send_prev(h).start()

    finish_prev(0, last_a(1, ba_sent))
    finish_prev(1, last_b(1, bb_sent))

    for c in started:
        c.wait_send()

    @pl.when(seg < n_seg - 1)
    def _():
        for h in range(2):
            send_next(h).wait_send()
            send_prev(h).wait_recv()

    @pl.when(seg > 0)
    def _():
        for h in range(2):
            send_prev(h).wait_send()
            send_next(h).wait_recv()


def settle(next_in, prev_in, next_out, prev_out):
    next_out[...] = next_in[...]
    prev_out[...] = prev_in[...]


def body(
    fwd_acts,
    fwd_ids,
    fwd_slots,
    bwd_acts,
    bwd_ids,
    bwd_slots,
    bwd_grad,
    norm_gain,
    router,
    w_gate,
    w_up,
    w_down,
):
    E = router.shape[2]
    per, D, F = w_gate.shape
    n_seg = lax.axis_size("segment")
    n_e = lax.axis_size("expert")
    n_t = lax.axis_size("token")
    tok = fwd_acts.shape[1]
    K = fwd_ids.shape[2]
    cap = max(2, min(3 * tok * K // (4 * E), tok - 1))
    W = D // n_t
    J = n_e // 2
    T = n_e * tok
    V = pltpu.VMEM
    dma = pltpu.SemaphoreType.DMA
    peers = max(J - 1, 1)
    toks = max(n_t - 1, 1)
    scratch = [
        V((3, 2, J, tok, D), bf16),
        V((2, J, tok, D), bf16),
        V((2, J, tok, 128), f32),
        V((per, F, D), bf16),
        V((per, F, D), bf16),
        V((per, F, D), bf16),
        V((per, T, F), bf16),
        V((per, T, F), bf16),
        V((per, T, F), bf16),
        V((2, 2, 2, n_t, J, tok, W // 2), bf16),
        V((2, 2, n_t, J, tok, W // 2), bf16),
        V((2, toks, J, tok, W // 2), bf16),
        V((2, toks, J, tok, W // 2), bf16),
        V((2, J, tok, W // 2), bf16),
        V((2, peers, tok, W // 2), bf16),
        V((2, peers, n_t, tok, W // 2), bf16),
        V((2, peers, n_t, tok, W // 2), bf16),
        V((2, n_t, tok, W // 2), bf16),
        V((2, toks, tok, W // 2), bf16),
        V((T, 128), f32),
        V((n_e, 8, tok), f32),
        V((n_e, n_t, 8, tok), f32),
        V((128, 128), f32),
        V((6, tok, 128), f32),
        V((tok, W), f32),
        V((2, tok, W), bf16),
        V((128, 128), f32),
        dma((3, per)),
        dma((3,)),
        dma((3,)),
        dma((3,)),
        dma((3, peers)),
        dma((3, peers)),
        dma((n_e - 1,)),
        dma((n_e - 1,)),
        dma((3, peers, n_t)),
        dma((3, peers, n_t)),
        dma((3, peers, toks)),
        dma((3, peers, toks)),
        dma((2, 2)),
        dma((2, 2)),
        dma((2, toks)),
        dma((2, toks)),
        dma((2, peers)),
        dma((2, peers)),
        dma((2, peers)),
        dma((2, peers)),
        dma((2, toks)),
        dma((2, toks)),
        dma((n_e, n_t)),
        dma((n_e, n_t)),
        dma((2, 2)),
        dma((2, 2)),
    ]
    codes = jnp.concatenate(
        [
            (ids[0] + jnp.where(slots[0] < cap, 0, E)).T
            for ids, slots in ((fwd_ids, fwd_slots), (bwd_ids, bwd_slots))
        ],
        axis=0,
    )
    vm = pl.BlockSpec(memory_space=pltpu.VMEM)
    hbm = pl.BlockSpec(memory_space=pl.ANY)
    out = jax.ShapeDtypeStruct((1, tok, W), bf16)
    sizes = (n_seg, n_e, n_t, per, E, tok, D, F, K)
    moved = pl.pallas_call(
        functools.partial(kernel, sizes),
        out_shape=(out, out),
        in_specs=[hbm] * 3 + [vm] * 3 + [hbm] * 3,
        out_specs=(vm, vm),
        scratch_shapes=scratch,
        compiler_params=pltpu.CompilerParams(
            collective_id=0, has_side_effects=True, vmem_limit_bytes=63 * 1024 * 1024
        ),
        name="relay_moe",
    )(
        fwd_acts,
        bwd_acts,
        bwd_grad,
        codes,
        norm_gain,
        router[0].T,
        jnp.swapaxes(w_gate, 1, 2),
        jnp.swapaxes(w_up, 1, 2),
        w_down,
    )
    return pl.pallas_call(
        settle, out_shape=(out, out), in_specs=[vm] * 2, out_specs=(vm, vm), name="settle"
    )(*moved)


def solution(mesh):
    return jax.shard_map(
        body,
        mesh=mesh,
        in_specs=(
            P("segment", "expert", None),
            P("segment", "expert", None),
            P("segment", "expert", None),
            P("segment", "expert", None),
            P("segment", "expert", None),
            P("segment", "expert", None),
            P("segment", "expert", None),
            P("segment", None),
            P("segment", None, None),
            P("expert", None, "token"),
            P("expert", None, "token"),
            P("expert", "token", None),
        ),
        out_specs=(P("segment", "expert", "token"), P("segment", "expert", "token")),
        check_vma=False,
    )
```
